512 devices in a mesh: tok: 32 (over z, y_lo), feat: 16 (over x, y_hi, core).
Axes of the slice: x: 4, y: 4 (y_hi: 2, y_lo: 2; y = y_hi * 2 + y_lo), z: 16, core: 2. Of those that a mesh axis runs over, the one named last changes fastest.
Arguments:
- tokens: bfloat16 [512, 12288], P('tok', 'feat'), may hold values from -6 to 6
- up_weight: bfloat16 [16, 3072, 5, 768], P('feat', 'tok'), may hold values from -0.09375 to 0.09375
- down_weight: bfloat16 [16, 3072, 5, 768], P('feat', 'tok'), may hold values from -0.046875 to 0.046875
- up_left: bfloat16 [12288, 512], P('feat'), may hold values from -0.0546875 to 0.0546875
- up_right: bfloat16 [16, 3072, 512], P('feat', 'tok'), may hold values from -0.25 to 0.25
- down_left: bfloat16 [16, 3072, 512], P('feat', 'tok'), may hold values from -0.02734375 to 0.02734375
- down_right: bfloat16 [512, 12288], P(None, 'feat'), may hold values from -0.25 to 0.25
Outputs:
- mixed: bfloat16 [512, 12288], P('tok', 'feat')
The draws below stay inside these ranges and needn't reach their ends.
All inputs are finite; a program needn't handle non-finite values.
Results may differ from the reference program's by a relative error of at most 0.0058.
Values may be sent and summed in bfloat16 or wider, within the bound.
No kernel may reach another device: no remote copies, remote signals or barrier semaphores. Data moves between devices by JAX's collectives and lax.ppermute only.
A program may use at most 64 MiB of HBM per device.

```python
import jax
import jax.numpy as jnp
import numpy as np
from jax import lax

D = 12288
FF = 49152
RANK = 512
TOKENS = 512
LEVELS = 4
DB = 768
FFB = 3072
N_FEAT = 16


def steps_of(rng, dims, cuts, low, top_value):
    factor_of, own = 1.0, jax.random.fold_in(rng, 6)
    for dim, shards_of in cuts:
        heights = jnp.exp(jax.random.uniform(jax.random.fold_in(own, dim), (shards_of,), jnp.float32, low / len(cuts), top_value / len(cuts)))
        factor_of = factor_of * jnp.repeat(heights, dims[dim] // shards_of).reshape([-1 if axis == dim else 1 for axis in range(len(dims))])
    return factor_of


def centred(rng, shape, deviation, bound, split=(), kind=jnp.bfloat16):
    entries = deviation * jax.random.normal(rng, shape, jnp.float32)
    if split:
        entries = entries * steps_of(rng, shape, split, -0.22, 0.18)
    return jnp.clip(entries, -bound, bound).astype(kind)


def setup_inputs(seed: int = 0) -> dict:
    arg_keys = jax.random.split(jax.random.key(seed), 8)
    return {
        "tokens": centred(arg_keys[0], (TOKENS, D), 1.0, 6.0, ((0, 32), (1, 16))),
        "up_weight": centred(arg_keys[1], (N_FEAT, FFB, LEVELS + 1, DB), ((LEVELS + 1) * DB) ** -0.5, 0.09375, ((0, 16), (1, 32))),
        "down_weight": centred(arg_keys[2], (N_FEAT, FFB, LEVELS + 1, DB), ((LEVELS + 1) * FFB) ** -0.5, 0.046875, ((0, 16), (1, 32))),
        "up_left": centred(arg_keys[3], (D, RANK), D ** -0.5, 0.0546875, ((0, 16),)),
        "up_right": centred(arg_keys[4], (N_FEAT, FFB, RANK), RANK ** -0.5, 0.25, ((0, 16), (1, 32))),
        "down_left": centred(arg_keys[5], (N_FEAT, FFB, RANK), FF ** -0.5, 0.02734375, ((0, 16), (1, 32))),
        "down_right": centred(arg_keys[6], (RANK, D), RANK ** -0.5, 0.25, ((1, 16),)),
    }


def reference(tokens, up_weight, down_weight, up_left, up_right, down_left, down_right):
    table = jnp.array(np.array([[i ^ ((1 << k) >> 1) for k in range(LEVELS + 1)] for i in range(N_FEAT)]), dtype=jnp.int32)
    count = tokens.shape[0]
    blocks = tokens.reshape(count, N_FEAT, DB)
    code = jnp.dot(tokens, up_left, preferred_element_type=jnp.float32).astype(jnp.bfloat16)

    def up_block(index):
        inputs = jnp.take(blocks, table[index], axis=1).reshape(count, (LEVELS + 1) * DB)
        weights = up_weight[index].reshape(FFB, (LEVELS + 1) * DB)
        return jnp.dot(inputs, weights.T, preferred_element_type=jnp.float32)

    pre = lax.map(up_block, jnp.arange(N_FEAT, dtype=jnp.int32))
    pre = jnp.transpose(pre, (1, 0, 2)).reshape(count, FF)
    pre = pre + jnp.dot(code, up_right.reshape(FF, RANK).T, preferred_element_type=jnp.float32)
    hidden = jax.nn.gelu(pre, approximate=False).astype(jnp.bfloat16)
    hblocks = hidden.reshape(count, N_FEAT, FFB)

    def down_block(total, index):
        source = jnp.take(hblocks, index, axis=1)
        part = jnp.dot(source, down_weight[index].reshape(FFB, (LEVELS + 1) * DB), preferred_element_type=jnp.float32)
        return total.at[:, table[index]].add(part.reshape(count, LEVELS + 1, DB)), None

    start_total = jnp.zeros((count, N_FEAT, DB), jnp.float32)
    total, unused = lax.scan(down_block, start_total, jnp.arange(N_FEAT, dtype=jnp.int32))
    back = jnp.dot(hidden, down_left.reshape(FF, RANK), preferred_element_type=jnp.float32).astype(jnp.bfloat16)
    mixed = total.reshape(count, D) + jnp.dot(back, down_right, preferred_element_type=jnp.float32)
    return mixed.astype(jnp.bfloat16)
```

```python
import jax
import jax.numpy as jnp
from jax import lax
from jax.sharding import Mesh, PartitionSpec as P


F32 = jnp.float32
BF16 = jnp.bfloat16
FEAT = ("x", "yh", "c")
LEVEL_AXES = (("c", 0), ("yh", 0), ("x", 0), ("x", 1))


def swap(array, axis, bit):
    return lax.ppermute(array, axis, [(i, i ^ (1 << bit)) for i in range(lax.axis_size(axis))])


def dot_nt(a, b):
    return lax.dot_general(a, b, (((1,), (1,)), ((), ())), preferred_element_type=F32)


def dot_nn(a, b):
    return lax.dot_general(a, b, (((1,), (0,)), ((), ())), preferred_element_type=F32)


def share(array, axis):
    n = lax.axis_size(axis)
    return lax.all_to_all(jnp.broadcast_to(array[None], (n,) + array.shape), axis, 0, 0, tiled=True)


def per_device(tokens, up_weight, down_weight, up_left, up_right, down_left, down_right):
    nz = lax.axis_size("z")
    count, db = tokens.shape
    rows, rank = up_right.shape[1:]
    kinds = up_weight.shape[2]
    up = up_weight[0].transpose(1, 0, 2).reshape(kinds * rows, db)
    down = down_weight[0].transpose(1, 0, 2).reshape(kinds * rows, db)

    code_part = dot_nn(tokens, up_left).astype(BF16)
    code = jnp.sum(share(code_part, FEAT).astype(F32), axis=0).astype(BF16)

    head = db - rank
    packed = jnp.concatenate(
        [
            up,
            down,
            jnp.concatenate([up_right[0], down_left[0][:, :head]], axis=1),
            jnp.concatenate([down_left[0][:, head:], jnp.zeros((rows, db - (rank - head)), BF16)], axis=1),
        ],
        axis=0,
    )
    packed, code = lax.optimization_barrier((packed, code))
    other = swap(packed, "yl", 0)
    gathered = lax.all_gather(jnp.concatenate([tokens, code], axis=1), "z", axis=0, tiled=True)
    own = gathered[:, :db]
    codes = gathered[:, db:]
    pieces = [own] + [swap(own, axis, bit) for axis, bit in LEVEL_AXES]

    n = kinds * rows
    up_o, down_o = other[:n], other[n : 2 * n]
    right_o = other[2 * n : 2 * n + rows, :rank]
    left_o = jnp.concatenate([other[2 * n : 2 * n + rows, rank:], other[2 * n + rows :, : rank - head]], axis=1)

    def pre_of(weight, right):
        total = dot_nt(codes, right)
        for k in range(kinds):
            total = total + dot_nt(pieces[k], weight[k * rows : (k + 1) * rows])
        return jax.nn.gelu(total, approximate=False).astype(BF16)

    h_a = pre_of(up, up_right[0])
    h_b = pre_of(up_o, right_o)

    def term(k):
        part = slice(k * rows, (k + 1) * rows)
        return dot_nn(h_a, down[part]) + dot_nn(h_b, down_o[part])

    sent = [swap(term(k + 1).astype(BF16), axis, bit) for k, (axis, bit) in enumerate(LEVEL_AXES)]
    back = (dot_nn(h_a, down_left[0]) + dot_nn(h_b, left_o)).astype(BF16)
    back = lax.all_to_all(back.reshape(nz, count, rank), "z", 0, 0, tiled=True)
    back = jnp.sum(back.astype(F32), axis=0).astype(BF16)
    back = jnp.sum(share(back, FEAT).astype(F32), axis=0).astype(BF16)

    total = term(0)
    for s in sent:
        total = total + s.astype(F32)
    total = lax.all_to_all(total.astype(BF16).reshape(nz, count, db), "z", 0, 0, tiled=True)
    total = jnp.sum(total.astype(F32), axis=0)
    return (total + dot_nn(back, down_right)).astype(BF16)


def solution(mesh):
    tok, feat = ("z", "yl"), FEAT
    inner = Mesh(mesh.devices.reshape(16, 2, 4, 2, 2), tok + feat)
    return jax.shard_map(
        per_device,
        mesh=inner,
        in_specs=(
            P(tok, feat),
            P(feat, tok, None, None),
            P(feat, tok, None, None),
            P(feat, None),
            P(feat, tok, None),
            P(feat, tok, None),
            P(None, feat),
        ),
        out_specs=P(tok, feat),
        check_vma=False,
    )
```

```python
import functools

import jax
import jax.numpy as jnp
from jax import lax
from jax.experimental import pallas as pl
from jax.experimental.pallas import tpu as pltpu
from jax.sharding import Mesh, PartitionSpec as P


F32 = jnp.float32
BF16 = jnp.bfloat16
FEAT = ("x", "yh", "c")
LEVEL_AXES = (("c", 0), ("yh", 0), ("x", 0), ("x", 1))


def swap(array, axis, bit):
    return lax.ppermute(array, axis, [(i, i ^ (1 << bit)) for i in range(lax.axis_size(axis))])


def dot_nt(a, b):
    return lax.dot_general(a, b, (((1,), (1,)), ((), ())), preferred_element_type=F32)


def dot_nn(a, b):
    return lax.dot_general(a, b, (((1,), (0,)), ((), ())), preferred_element_type=F32)


def share(array, axis):
    n = lax.axis_size(axis)
    return lax.all_to_all(jnp.broadcast_to(array[None], (n,) + array.shape), axis, 0, 0, tiled=True)


def total_of(stack):
    return lax.reduce_precision(jnp.sum(stack.astype(F32), axis=0), 8, 7).astype(BF16)


def sum_over_feat(part, n):
    part = lax.all_to_all(part.reshape((n, part.shape[0] // n) + part.shape[1:]), FEAT, 0, 0, tiled=True)
    group = total_of(part)
    whole = share(group, FEAT)
    return whole.reshape((-1,) + group.shape[1:])


def ffn_body(kinds, rows, db, rank, x0, x1, x2, x3, x4, code, up, right, down, left, other, t0, t1, t2, t3, t4, back):
    n = kinds * rows
    head = db - rank
    xs = (x0, x1, x2, x3, x4)

    def pair(ref, base, k):
        lo = k * rows
        return jnp.concatenate([ref[lo : lo + rows, :], other[base + lo : base + lo + rows, :]], axis=0)

    pre = dot_nt(code[...], jnp.concatenate([right[...], other[2 * n : 2 * n + rows, :rank]], axis=0))
    for k in range(kinds):
        pre = pre + dot_nt(xs[k][...], pair(up, 0, k))
    hidden = (0.5 * pre * (1.0 + lax.erf(pre * (0.5**0.5)))).astype(BF16)
    outs = (t0, t1, t2, t3, t4)
    for k in (2, 3, 4, 1, 0):
        outs[k][...] = dot_nn(hidden, pair(down, n, k)).astype(outs[k].dtype)
    low = jnp.concatenate([left[:, :head], other[2 * n : 2 * n + rows, rank:]], axis=0)
    high = jnp.concatenate([left[:, head:], other[2 * n + rows :, : rank - head]], axis=0)
    back[:, :head] = dot_nn(hidden, low).astype(BF16)
    back[:, head:] = dot_nn(hidden, high).astype(BF16)


def ffn_call(pieces, code, up, right, down, left, other):
    count = code.shape[0]
    rows, rank = right.shape
    db = up.shape[1]
    kinds = up.shape[0] // rows
    shapes = [jax.ShapeDtypeStruct((count, db), F32)]
    shapes += [jax.ShapeDtypeStruct((count, db), BF16)] * (kinds - 1)
    shapes += [jax.ShapeDtypeStruct((count, rank), BF16)]
    return pl.pallas_call(
        functools.partial(ffn_body, kinds, rows, db, rank),
        out_shape=shapes,
        compiler_params=pltpu.CompilerParams(vmem_limit_bytes=16 * 2**20),
        name="ffn",
    )(*pieces, code, up, right, down, left, other)


def per_device(tokens, up_weight, down_weight, up_left, up_right, down_left, down_right):
    nz, nf = lax.axis_size("z"), lax.axis_size(FEAT)
    count, db = tokens.shape
    rows, rank = up_right.shape[1:]
    kinds = up_weight.shape[2]
    up = up_weight[0].transpose(1, 0, 2).reshape(kinds * rows, db)
    down = down_weight[0].transpose(1, 0, 2).reshape(kinds * rows, db)

    head = db - rank
    packed = jnp.concatenate(
        [
            up,
            down,
            jnp.concatenate([up_right[0], down_left[0][:, :head]], axis=1),
            jnp.concatenate([down_left[0][:, head:], jnp.zeros((rows, db - (rank - head)), BF16)], axis=1),
        ],
        axis=0,
    )
    other = swap(packed, "yl", 0)
    own = lax.all_gather(tokens, "z", axis=0, tiled=True)
    code = sum_over_feat(dot_nn(own, up_left).astype(BF16), nf)
    pieces = [own]
    for axis, bit in LEVEL_AXES:
        pieces.append(swap(own, axis, bit))

    own_total, *terms, back = ffn_call(pieces, code, up, up_right[0], down, down_left[0], other)
    back = sum_over_feat(back, nf)
    sent = []
    for part, (axis, bit) in zip(terms, LEVEL_AXES):
        sent.append(swap(part, axis, bit))
    total = own_total + dot_nn(back, down_right)
    for s in sent:
        total = total + s.astype(F32)
    total = total.astype(BF16)
    total = lax.all_to_all(total.reshape(nz, count, db), "z", 0, 0, tiled=True)
    return total_of(total)


def solution(mesh):
    tok, feat = ("z", "yl"), FEAT
    inner = Mesh(mesh.devices.reshape(16, 2, 4, 2, 2), tok + feat)
    return jax.shard_map(
        per_device,
        mesh=inner,
        in_specs=(
            P(tok, feat),
            P(feat, tok, None, None),
            P(feat, tok, None, None),
            P(feat, None),
            P(feat, tok, None),
            P(feat, tok, None),
            P(None, feat),
        ),
        out_specs=P(tok, feat),
        check_vma=False,
    )
```

```python
import functools

import jax
import jax.numpy as jnp
from jax import lax
from jax.experimental import pallas as pl
from jax.experimental.pallas import tpu as pltpu
from jax.sharding import Mesh, PartitionSpec as P


F32 = jnp.float32
BF16 = jnp.bfloat16
FEAT = ("x", "yh", "c")
UP_MIB = 24
DOWN_MIB = 60
LEVEL_AXES = (("c", 0), ("yh", 0), ("x", 0), ("x", 1))


def swap(array, axis, bit):
    return lax.ppermute(array, axis, [(i, i ^ (1 << bit)) for i in range(lax.axis_size(axis))])


def dot_nt(a, b):
    return lax.dot_general(a, b, (((1,), (1,)), ((), ())), preferred_element_type=F32)


def dot_nn(a, b):
    return lax.dot_general(a, b, (((1,), (0,)), ((), ())), preferred_element_type=F32)


def share(array, axis):
    n = lax.axis_size(axis)
    return lax.all_to_all(jnp.broadcast_to(array[None], (n,) + array.shape), axis, 0, 0, tiled=True)


def total_of(stack):
    return lax.reduce_precision(jnp.sum(stack.astype(F32), axis=0), 8, 7).astype(BF16)


def sum_over_feat(part, n):
    part = lax.all_to_all(part.reshape((n, part.shape[0] // n) + part.shape[1:]), FEAT, 0, 0, tiled=True)
    group = total_of(part)
    whole = share(group, FEAT)
    return whole.reshape((-1,) + group.shape[1:])


def fetch(src, dst, sem, lo, size):
    part = pl.ds(lo, size)
    return pltpu.make_async_copy(src.at[part], dst.at[part], sem)


def pair(mine, other, rows, base, k):
    lo = k * rows
    return jnp.concatenate([mine[lo : lo + rows, :], other[base + lo : base + lo + rows, :]], axis=0)


def up_body(kinds, rows, db, rank, *refs):
    n = kinds * rows
    head = db - rank
    count = kinds + 4
    ins, (hidden_out, back) = refs[:count], refs[count : count + 2]
    bufs, sems = refs[count + 2 : -1], refs[-1]
    xs, (up, right, left, other) = bufs[:kinds], bufs[kinds:]

    def whole(i):
        return fetch(ins[i], bufs[i], sems.at[i], 0, ins[i].shape[0])

    last = count - 1
    first = [
        whole(0),
        whole(kinds + 1),
        fetch(ins[last], other, sems.at[last], 2 * n, 2 * rows),
        whole(kinds),
        fetch(ins[last], other, sems.at[last + 1], 0, n),
    ]
    partners = [whole(i) for i in range(1, kinds)]
    late = whole(kinds + 2)
    for copy in first + partners + [late]:
        copy.start()
    for copy in first:
        copy.wait()
    pre = dot_nt(xs[0][:, db:], jnp.concatenate([right[...], other[2 * n : 2 * n + rows, :rank]], axis=0))
    pre = pre + dot_nt(xs[0][:, :db], pair(up, other, rows, 0, 0))
    for k in range(1, kinds):
        partners[k - 1].wait()
        pre = pre + dot_nt(xs[k][...], pair(up, other, rows, 0, k))
    hidden = (0.5 * pre * (1.0 + lax.erf(pre * (0.5**0.5)))).astype(BF16)
    hidden_out[...] = hidden
    late.wait()
    low = jnp.concatenate([left[:, :head], other[2 * n : 2 * n + rows, rank:]], axis=0)
    high = jnp.concatenate([left[:, head:], other[2 * n + rows :, : rank - head]], axis=0)
    back[:, :head] = dot_nn(hidden, low).astype(BF16)
    back[:, head:] = dot_nn(hidden, high).astype(BF16)


def up_call(gathered, pieces, up, right, left, other):
    count = gathered.shape[0]
    rows, rank = right.shape
    db = up.shape[1]
    kinds = up.shape[0] // rows
    args = (gathered, *pieces, up, right, left, other)
    return pl.pallas_call(
        functools.partial(up_body, kinds, rows, db, rank),
        out_shape=[jax.ShapeDtypeStruct((count, 2 * rows), BF16), jax.ShapeDtypeStruct((count, rank), BF16)],
        in_specs=[pl.BlockSpec(memory_space=pl.ANY)] * len(args),
        scratch_shapes=[pltpu.VMEM(a.shape, BF16) for a in args] + [pltpu.SemaphoreType.DMA((len(args) + 1,))],
        compiler_params=pltpu.CompilerParams(vmem_limit_bytes=UP_MIB * 2**20),
        name="ffn_up",
    )(*args)


def down_body(kinds, rows, hidden_in, down_in, other_in, *refs):
    n = kinds * rows
    outs, (hidden, down, other) = refs[:kinds], refs[kinds : kinds + 3]
    stage, (in_sems, out_sems) = refs[kinds + 3 : -2], refs[-2:]
    head = fetch(hidden_in, hidden, in_sems.at[2 * kinds], 0, hidden.shape[0])
    head.start()
    order = (2, 4, 3, 1, 0)
    loads = {}
    for k in order:
        loads[k] = (
            fetch(down_in, down, in_sems.at[2 * k], k * rows, rows),
            fetch(other_in, other, in_sems.at[2 * k + 1], n + k * rows, rows),
        )
        for copy in loads[k]:
            copy.start()
    head.wait()
    stores = []
    for k in order:
        for copy in loads[k]:
            copy.wait()
        stage[k][...] = dot_nn(hidden[...], pair(down, other, rows, n, k)).astype(outs[k].dtype)
        stores.append(pltpu.make_async_copy(stage[k], outs[k], out_sems.at[k]))
        stores[-1].start()
    for copy in stores:
        copy.wait()


def down_call(hidden, down, other):
    count, db = hidden.shape[0], down.shape[1]
    rows = hidden.shape[1] // 2
    kinds = down.shape[0] // rows
    shapes = [jax.ShapeDtypeStruct((count, db), F32)]
    shapes += [jax.ShapeDtypeStruct((count, db), BF16)] * (kinds - 1)
    return pl.pallas_call(
        functools.partial(down_body, kinds, rows),
        out_shape=shapes,
        in_specs=[pl.BlockSpec(memory_space=pl.ANY)] * 3,
        out_specs=[pl.BlockSpec(memory_space=pl.ANY)] * kinds,
        scratch_shapes=[pltpu.VMEM(a.shape, BF16) for a in (hidden, down, other)]
        + [pltpu.VMEM(a.shape, a.dtype) for a in shapes]
        + [pltpu.SemaphoreType.DMA((2 * kinds + 1,)), pltpu.SemaphoreType.DMA((kinds,))],
        compiler_params=pltpu.CompilerParams(vmem_limit_bytes=DOWN_MIB * 2**20),
        name="ffn_down",
    )(hidden, down, other)


def code_body(x, w, stack):
    part = dot_nn(x[...], w[...]).astype(BF16)
    for i in range(stack.shape[0]):
        stack[i] = part


def code_call(tokens, up_left, n):
    shape = jax.ShapeDtypeStruct((n, tokens.shape[0], up_left.shape[1]), BF16)
    return pl.pallas_call(code_body, out_shape=shape, name="code_part", compiler_params=pltpu.CompilerParams(vmem_limit_bytes=8 * 2**20))(tokens, up_left)


def per_device(tokens, up_weight, down_weight, up_left, up_right, down_left, down_right):
    nz, nf = lax.axis_size("z"), lax.axis_size(FEAT)
    count, db = tokens.shape
    rows, rank = up_right.shape[1:]
    kinds = up_weight.shape[2]
    up = up_weight[0].transpose(1, 0, 2).reshape(kinds * rows, db)
    down = down_weight[0].transpose(1, 0, 2).reshape(kinds * rows, db)

    head = db - rank
    packed = jnp.concatenate(
        [
            up,
            down,
            jnp.concatenate([up_right[0], down_left[0][:, :head]], axis=1),
            jnp.concatenate([down_left[0][:, head:], jnp.zeros((rows, db - (rank - head)), BF16)], axis=1),
        ],
        axis=0,
    )
    stack = code_call(tokens, up_left, nf)
    stack = lax.all_to_all(stack, FEAT, 0, 0, tiled=True)
    other = swap(packed, "yl", 0)
    mine = jnp.concatenate([tokens, total_of(stack)], axis=1)
    gathered = lax.all_gather(mine, "z", axis=0, tiled=True)
    own = gathered[:, :db]
    pieces = []
    for axis, bit in LEVEL_AXES:
        pieces.append(swap(own, axis, bit))

    hidden, back = up_call(gathered, pieces, up, up_right[0], down_left[0], other)
    back = sum_over_feat(back, nf)
    own_total, *terms = down_call(hidden, down, other)
    sent = []
    for part, (axis, bit) in zip(terms, LEVEL_AXES):
        sent.append(swap(part, axis, bit))
    total = own_total + dot_nn(back, down_right)
    for s in sent:
        total = total + s.astype(F32)
    total = total.astype(BF16)
    total = lax.all_to_all(total.reshape(nz, count, db), "z", 0, 0, tiled=True)
    return total_of(total)


def solution(mesh):
    tok, feat = ("z", "yl"), FEAT
    inner = Mesh(mesh.devices.reshape(16, 2, 4, 2, 2), tok + feat)
    return jax.shard_map(
        per_device,
        mesh=inner,
        in_specs=(
            P(tok, feat),
            P(feat, tok, None, None),
            P(feat, tok, None, None),
            P(feat, None),
            P(feat, tok, None),
            P(feat, tok, None),
            P(None, feat),
        ),
        out_specs=P(tok, feat),
        check_vma=False,
    )
```

```python
import functools

import jax
import jax.numpy as jnp
from jax import lax
from jax.experimental import pallas as pl
from jax.experimental.pallas import tpu as pltpu
from jax.sharding import Mesh, PartitionSpec as P


F32 = jnp.float32
BF16 = jnp.bfloat16
FEAT = ("x", "yh", "c")
NEAR = 3
UP_MIB = 24
DOWN_MIB = 24
LEVEL_AXES = (("c", 0), ("yh", 0), ("x", 0), ("x", 1))


def swap(array, axis, bit):
    return lax.ppermute(array, axis, [(i, i ^ (1 << bit)) for i in range(lax.axis_size(axis))])


def dot_nt(a, b):
    return lax.dot_general(a, b, (((1,), (1,)), ((), ())), preferred_element_type=F32)


def dot_nn(a, b):
    return lax.dot_general(a, b, (((1,), (0,)), ((), ())), preferred_element_type=F32)


def share(array, axis):
    n = lax.axis_size(axis)
    return lax.all_to_all(jnp.broadcast_to(array[None], (n,) + array.shape), axis, 0, 0, tiled=True)


def total_of(stack):
    return lax.reduce_precision(jnp.sum(stack.astype(F32), axis=0), 8, 7).astype(BF16)


def sum_over_feat(part, n):
    part = lax.all_to_all(part.reshape((n, part.shape[0] // n) + part.shape[1:]), FEAT, 0, 0, tiled=True)
    group = total_of(part)
    whole = share(group, FEAT)
    return whole.reshape((-1,) + group.shape[1:])


def fetch(src, dst, sem, lo, size):
    part = pl.ds(lo, size)
    return pltpu.make_async_copy(src.at[part], dst.at[part], sem)


def pair(mine, other, rows, base, k):
    lo = base + k * rows
    return jnp.concatenate([ref[lo : lo + rows, :] for ref in (mine, other)], axis=0)


def up_body(kinds, rows, rank, *refs):
    n = kinds * rows
    count = kinds + 2
    ins, (hidden_out, back_out) = refs[:count], refs[count : count + 2]
    bufs, (staged, back, sems, out_sems) = refs[count + 2 : -4], refs[-4:]
    xs, (mine, other) = bufs[:kinds], bufs[kinds:]
    db = mine.shape[1]
    head = db - rank

    def whole(i):
        return fetch(ins[i], bufs[i], sems.at[i], 0, ins[i].shape[0])

    first = [whole(0)]
    for i in (kinds, kinds + 1):
        first.append(fetch(ins[i], bufs[i], sems.at[i], 2 * n, 2 * rows))
        first.append(fetch(ins[i], bufs[i], sems.at[i + 2], 0, n))
    partners = [whole(i) for i in range(1, kinds)]
    for copy in first + partners:
        copy.start()
    for copy in first:
        copy.wait()

    def both(lo, hi, at, size):
        return jnp.concatenate([ref[lo:hi, at : at + size] for ref in (mine, other)], axis=0)

    pre = dot_nt(xs[0][:, db:], both(2 * n, 2 * n + rows, 0, rank))
    pre = pre + dot_nt(xs[0][:, :db], pair(mine, other, rows, 0, 0))
    for k in range(1, kinds):
        partners[k - 1].wait()
        pre = pre + dot_nt(xs[k][...], pair(mine, other, rows, 0, k))
    hidden = (0.5 * pre * (1.0 + lax.erf(pre * (0.5**0.5)))).astype(BF16)
    staged[...] = hidden
    stores = [pltpu.make_async_copy(staged, hidden_out, out_sems.at[0])]
    stores[0].start()
    back[:, :head] = dot_nn(hidden, both(2 * n, 2 * n + rows, rank, head)).astype(BF16)
    back[:, head:] = dot_nn(hidden, both(2 * n + rows, 2 * n + 2 * rows, 0, rank - head)).astype(BF16)
    stores.append(pltpu.make_async_copy(back, back_out, out_sems.at[1]))
    stores[1].start()
    for copy in stores:
        copy.wait()


def up_call(gathered, pieces, mine, other, kinds):
    count, width = gathered.shape
    db = mine.shape[1]
    rank = width - db
    rows = mine.shape[0] // (2 * kinds + 2)
    args = (gathered, *pieces, mine, other)
    return pl.pallas_call(
        functools.partial(up_body, kinds, rows, rank),
        out_shape=[pltpu.HBM((count, 2 * rows), BF16), pltpu.HBM((count, rank), BF16)],
        in_specs=[pl.BlockSpec(memory_space=pl.ANY)] * len(args),
        scratch_shapes=[pltpu.VMEM(a.shape, BF16) for a in args]
        + [pltpu.VMEM((count, 2 * rows), BF16), pltpu.VMEM((count, rank), BF16)]
        + [pltpu.SemaphoreType.DMA((len(args) + 2,)), pltpu.SemaphoreType.DMA((2,))],
        compiler_params=pltpu.CompilerParams(vmem_limit_bytes=UP_MIB * 2**20),
        name="ffn_up",
    )(*args)


def down_body(kinds, near, rows, hidden_in, *refs):
    n = kinds * rows
    far = kinds - near
    far_in, (mine_in, other_in), refs = refs[:far], refs[far : far + 2], refs[far + 2 :]
    outs, refs = refs[:near], refs[near:]
    (hidden, *far_hidden), (mine, other), refs = refs[: far + 1], refs[far + 1 : far + 3], refs[far + 3 :]
    stage, (in_sems, out_sems) = refs[:near], refs[near:]
    given = [
        fetch(src, dst, in_sems.at[2 * kinds + i], 0, dst.shape[0])
        for i, (src, dst) in enumerate(zip((hidden_in, *far_in), (hidden, *far_hidden)))
    ]
    loads = {}
    given[0].start()
    for k in (*range(near - 1, -1, -1), *range(near, kinds)):
        loads[k] = (
            fetch(mine_in, mine, in_sems.at[2 * k], n + k * rows, rows),
            fetch(other_in, other, in_sems.at[2 * k + 1], n + k * rows, rows),
        )
        for copy in loads[k]:
            copy.start()
    for copy in given[1:]:
        copy.start()
    given[0].wait()
    stores = []
    for k in range(near - 1, -1, -1):
        for copy in loads[k]:
            copy.wait()
        part = dot_nn(hidden[...], pair(mine, other, rows, n, k))
        if k == 0:
            for i in range(far):
                given[i + 1].wait()
                for copy in loads[near + i]:
                    copy.wait()
                part = part + dot_nn(far_hidden[i][...], pair(mine, other, rows, n, near + i))
        stage[k][...] = part.astype(outs[k].dtype)
        stores.append(pltpu.make_async_copy(stage[k], outs[k], out_sems.at[k]))
        stores[-1].start()
    for copy in stores:
        copy.wait()


def down_call(hidden, far_hidden, mine, other, kinds):
    count, db = hidden.shape[0], mine.shape[1]
    rows = hidden.shape[1] // 2
    near = kinds - len(far_hidden)
    kept = [((count, db), F32)] + [((count, db), BF16)] * (near - 1)
    args = (hidden, *far_hidden, mine, other)
    return pl.pallas_call(
        functools.partial(down_body, kinds, near, rows),
        out_shape=[pltpu.HBM(*a) for a in kept],
        in_specs=[pl.BlockSpec(memory_space=pl.ANY)] * len(args),
        scratch_shapes=[pltpu.VMEM(a.shape, BF16) for a in args]
        + [pltpu.VMEM(*a) for a in kept]
        + [pltpu.SemaphoreType.DMA((2 * kinds + 1 + len(far_hidden),)), pltpu.SemaphoreType.DMA((near,))],
        compiler_params=pltpu.CompilerParams(vmem_limit_bytes=DOWN_MIB * 2**20),
        name="ffn_down",
    )(*args)


def pack_body(near_rows, rank, up, down, *refs):
    far, (right, left), out, sems = refs[:-4], refs[-4:-2], refs[-2], refs[-1]
    n, db = up.shape
    rows = right.shape[0]
    head = db - rank
    moves = [
        (up, out.at[pl.ds(0, n)]),
        (down.at[pl.ds(0, near_rows)], out.at[pl.ds(n, near_rows)]),
        (right, out.at[pl.ds(2 * n, rows), pl.ds(0, rank)]),
        (left.at[:, pl.ds(0, head)], out.at[pl.ds(2 * n, rows), pl.ds(rank, head)]),
        (left.at[:, pl.ds(head, rank - head)], out.at[pl.ds(2 * n + rows, rows), pl.ds(0, rank - head)]),
    ]
    moves += [(piece, out.at[pl.ds(n + near_rows + i * rows, rows)]) for i, piece in enumerate(far)]
    copies = [pltpu.make_async_copy(src, dst, sems.at[i]) for i, (src, dst) in enumerate(moves)]
    for copy in copies:
        copy.start()
    for copy in copies:
        copy.wait()


def pack_call(up, down, far, right, left):
    (n, db), (rows, rank) = up.shape, right.shape
    near_rows = n - len(far) * rows
    args = (up, down, *far, right, left)
    return pl.pallas_call(
        functools.partial(pack_body, near_rows, rank),
        out_shape=pltpu.HBM((2 * n + 2 * rows, db), BF16),
        in_specs=[pl.BlockSpec(memory_space=pl.ANY)] * len(args),
        scratch_shapes=[pltpu.SemaphoreType.DMA((5 + len(far),))],
        compiler_params=pltpu.CompilerParams(vmem_limit_bytes=60 * 2**20),
        name="pack",
    )(*args)


def code_body(x, w, stack):
    part = dot_nn(x[...], w[...]).astype(BF16)
    for i in range(stack.shape[0]):
        stack[i] = part


def code_call(tokens, up_left, n):
    shape = jax.ShapeDtypeStruct((n, tokens.shape[0], up_left.shape[1]), BF16)
    return pl.pallas_call(code_body, out_shape=shape, name="code_part", compiler_params=pltpu.CompilerParams(vmem_limit_bytes=60 * 2**20))(tokens, up_left)


def per_device(tokens, up_weight, down_weight, up_left, up_right, down_left, down_right):
    nz, nf = lax.axis_size("z"), lax.axis_size(FEAT)
    count, db = tokens.shape
    rows, _ = up_right.shape[1:]
    kinds = up_weight.shape[2]
    up = up_weight[0].transpose(1, 0, 2).reshape(kinds * rows, db)
    down = down_weight[0].transpose(1, 0, 2).reshape(kinds * rows, db)

    far = []
    for k in range(NEAR, kinds):
        axis, bit = LEVEL_AXES[k - 1]
        far.append(swap(down[k * rows : (k + 1) * rows], axis, bit))

    packed = pack_call(up, down, far, up_right[0], down_left[0])
    stack = code_call(tokens, up_left, nf)
    stack = lax.all_to_all(stack, FEAT, 0, 0, tiled=True)
    other = swap(packed, "yl", 0)
    mine = jnp.concatenate([tokens, total_of(stack)], axis=1)
    gathered = lax.all_gather(mine, "z", axis=0, tiled=True)
    own = gathered[:, :db]
    pieces = []
    for axis, bit in LEVEL_AXES:
        pieces.append(swap(own, axis, bit))

    hidden, back = up_call(gathered, pieces, packed, other, kinds)
    back = sum_over_feat(back, nf)
    far_hidden = []
    for axis, bit in LEVEL_AXES[NEAR - 1 :]:
        far_hidden.append(swap(hidden, axis, bit))
    own_total, *terms = down_call(hidden, far_hidden, packed, other, kinds)
    sent = []
    for part, (axis, bit) in zip(terms, LEVEL_AXES):
        sent.append(swap(part, axis, bit))
    total = own_total + dot_nn(back, down_right)
    for s in sent:
        total = total + s.astype(F32)
    total = total.astype(BF16)
    total = lax.all_to_all(total.reshape(nz, count, db), "z", 0, 0, tiled=True)
    return total_of(total)


def solution(mesh):
    tok, feat = ("z", "yl"), FEAT
    inner = Mesh(mesh.devices.reshape(16, 2, 4, 2, 2), tok + feat)
    return jax.shard_map(
        per_device,
        mesh=inner,
        in_specs=(
            P(tok, feat),
            P(feat, tok, None, None),
            P(feat, tok, None, None),
            P(feat, None),
            P(feat, tok, None),
            P(feat, tok, None),
            P(None, feat),
        ),
        out_specs=P(tok, feat),
        check_vma=False,
    )
```

```python
import functools

import jax
import jax.numpy as jnp
from jax import lax
from jax.experimental import pallas as pl
from jax.experimental.pallas import tpu as pltpu
from jax.sharding import Mesh, PartitionSpec as P


F32 = jnp.float32
BF16 = jnp.bfloat16
FEAT = ("x", "yh", "c")
FFN_MIB = 24
LEVEL_AXES = (("c", 0), ("yh", 0), ("x", 0), ("x", 1))


def swap(array, axis, bit):
    return lax.ppermute(array, axis, [(i, i ^ (1 << bit)) for i in range(lax.axis_size(axis))])


def dot_nt(a, b):
    return lax.dot_general(a, b, (((1,), (1,)), ((), ())), preferred_element_type=F32)


def dot_nn(a, b):
    return lax.dot_general(a, b, (((1,), (0,)), ((), ())), preferred_element_type=F32)


def total_of(stack):
    return lax.reduce_precision(jnp.sum(stack.astype(F32), axis=0), 8, 7).astype(BF16)


def fetch(src, dst, sem, lo, size):
    part = pl.ds(lo, size)
    return pltpu.make_async_copy(src.at[part], dst.at[part], sem)


def ffn_body(kinds, rows, rank, *refs):
    n = kinds * rows
    count = kinds + 2
    ins, outs = refs[:count], refs[count : count + kinds + 1]
    bufs, stage = refs[count + kinds + 1 : 2 * count + kinds + 1], refs[2 * count + kinds + 1 : -2]
    sems, out_sems = refs[-2:]
    xs, (mine, other) = bufs[:kinds], bufs[kinds:]
    db = mine.shape[1]
    head = db - rank

    def part(i, sem, lo, size):
        return fetch(ins[i], bufs[i], sems.at[sem], lo, size)

    def stored(k):
        copy = pltpu.make_async_copy(stage[k], outs[k], out_sems.at[k])
        copy.start()
        return copy

    first = [part(0, 0, 0, xs[0].shape[0])]
    late = []
    for i in (kinds, kinds + 1):
        first.append(part(i, i, 2 * n, 2 * rows))
        first.append(part(i, i + 2, 0, n))
        late.append(part(i, i + 4, n, n))
    partners = [part(i, i, 0, xs[i].shape[0]) for i in range(1, kinds)]
    for copy in first + partners + late:
        copy.start()
    for copy in first:
        copy.wait()

    def both(lo, hi, at, size):
        return jnp.concatenate([ref[lo:hi, at : at + size] for ref in (mine, other)], axis=0)

    pre = dot_nt(xs[0][:, db:], both(2 * n, 2 * n + rows, 0, rank))
    pre = pre + dot_nt(xs[0][:, :db], both(0, rows, 0, db))
    for k in range(1, kinds):
        partners[k - 1].wait()
        pre = pre + dot_nt(xs[k][...], both(k * rows, (k + 1) * rows, 0, db))
    hidden = (0.5 * pre * (1.0 + lax.erf(pre * (0.5**0.5)))).astype(BF16)
    back = stage[kinds]
    back[:, :head] = dot_nn(hidden, both(2 * n, 2 * n + rows, rank, head)).astype(BF16)
    back[:, head:] = dot_nn(hidden, both(2 * n + rows, 2 * n + 2 * rows, 0, rank - head)).astype(BF16)
    stores = [stored(kinds)]
    for copy in late:
        copy.wait()
    for k in range(kinds):
        lo = n + k * rows
        stage[k][...] = dot_nn(hidden, both(lo, lo + rows, 0, db)).astype(outs[k].dtype)
        stores.append(stored(k))
    for copy in stores:
        copy.wait()


def ffn_call(gathered, pieces, mine, other, kinds):
    count, width = gathered.shape
    db = mine.shape[1]
    rank = width - db
    rows = mine.shape[0] // (2 * kinds + 2)
    args = (gathered, *pieces, mine, other)
    outs = [((count, db), F32)] + [((count, db), BF16)] * (kinds - 1) + [((count, rank), BF16)]
    return pl.pallas_call(
        functools.partial(ffn_body, kinds, rows, rank),
        out_shape=[pltpu.HBM(*a) for a in outs],
        in_specs=[pl.BlockSpec(memory_space=pl.ANY)] * len(args),
        scratch_shapes=[pltpu.VMEM(a.shape, BF16) for a in args]
        + [pltpu.VMEM(*a) for a in outs]
        + [pltpu.SemaphoreType.DMA((len(args) + 4,)), pltpu.SemaphoreType.DMA((len(outs),))],
        compiler_params=pltpu.CompilerParams(vmem_limit_bytes=FFN_MIB * 2**20),
        name="ffn",
    )(*args)


def pack_body(rank, up, down, right, left, out, sems):
    n, db = up.shape
    rows = right.shape[0]
    head = db - rank
    moves = (
        (up, out.at[pl.ds(0, n)]),
        (down, out.at[pl.ds(n, n)]),
        (right, out.at[pl.ds(2 * n, rows), pl.ds(0, rank)]),
        (left.at[:, pl.ds(0, head)], out.at[pl.ds(2 * n, rows), pl.ds(rank, head)]),
        (left.at[:, pl.ds(head, rank - head)], out.at[pl.ds(2 * n + rows, rows), pl.ds(0, rank - head)]),
    )
    copies = [pltpu.make_async_copy(src, dst, sems.at[i]) for i, (src, dst) in enumerate(moves)]
    for copy in copies:
        copy.start()
    for copy in copies:
        copy.wait()


def pack_call(up, down, right, left):
    (n, db), (rows, rank) = up.shape, right.shape
    return pl.pallas_call(
        functools.partial(pack_body, rank),
        out_shape=pltpu.HBM((2 * n + 2 * rows, db), BF16),
        in_specs=[pl.BlockSpec(memory_space=pl.ANY)] * 4,
        scratch_shapes=[pltpu.SemaphoreType.DMA((5,))],
        compiler_params=pltpu.CompilerParams(vmem_limit_bytes=60 * 2**20),
        name="pack",
    )(up, down, right, left)


def code_body(x, w, stack):
    part = dot_nn(x[...], w[...]).astype(BF16)
    for i in range(stack.shape[0]):
        stack[i] = part


def code_call(tokens, up_left, n):
    shape = jax.ShapeDtypeStruct((n, tokens.shape[0], up_left.shape[1]), BF16)
    return pl.pallas_call(code_body, out_shape=shape, name="code_part", compiler_params=pltpu.CompilerParams(vmem_limit_bytes=60 * 2**20))(tokens, up_left)


def per_device(tokens, up_weight, down_weight, up_left, up_right, down_left, down_right):
    nz, nf = lax.axis_size("z"), lax.axis_size(FEAT)
    count, db = tokens.shape
    rows, rank = up_right.shape[1:]
    kinds = up_weight.shape[2]
    up = up_weight[0].transpose(1, 0, 2).reshape(kinds * rows, db)
    down = down_weight[0].transpose(1, 0, 2).reshape(kinds * rows, db)

    packed = pack_call(up, down, up_right[0], down_left[0])
    stack = code_call(tokens, up_left, nf)
    stack = lax.all_to_all(stack, FEAT, 0, 0, tiled=True)
    other = swap(packed, "yl", 0)
    mine = jnp.concatenate([tokens, total_of(stack)], axis=1)
    gathered = lax.all_gather(mine, "z", axis=0, tiled=True)
    own = gathered[:, :db]
    pieces = []
    for axis, bit in LEVEL_AXES:
        pieces.append(swap(own, axis, bit))

    own_total, *terms, back = ffn_call(gathered, pieces, packed, other, kinds)
    sent = []
    for part, (axis, bit) in zip(terms, LEVEL_AXES):
        sent.append(swap(part, axis, bit))
    back = lax.all_to_all(back.reshape(nz, count, rank), "z", 0, 0, tiled=True)
    total = own_total
    for s in sent:
        total = total + s.astype(F32)
    total = total.astype(BF16)
    total = lax.all_to_all(total.reshape(nz, count, db), "z", 0, 0, tiled=True)
    back = total_of(back)
    back = lax.all_gather(back, FEAT, axis=0)
    back = total_of(back)
    total = jnp.sum(total.astype(F32), axis=0)
    return (total + dot_nn(back, down_right)).astype(BF16)


def solution(mesh):
    tok, feat = ("z", "yl"), FEAT
    inner = Mesh(mesh.devices.reshape(16, 2, 4, 2, 2), tok + feat)
    return jax.shard_map(
        per_device,
        mesh=inner,
        in_specs=(
            P(tok, feat),
            P(feat, tok, None, None),
            P(feat, tok, None, None),
            P(feat, None),
            P(feat, tok, None),
            P(feat, tok, None),
            P(None, feat),
        ),
        out_specs=P(tok, feat),
        check_vma=False,
    )
```

```python
import functools

import jax
import jax.numpy as jnp
from jax import lax
from jax.experimental import pallas as pl
from jax.experimental.pallas import tpu as pltpu
from jax.sharding import Mesh, PartitionSpec as P


F32 = jnp.float32
BF16 = jnp.bfloat16
FEAT = ("x", "yh", "c")
FFN_MIB = 24
LEVEL_AXES = (("c", 0), ("yh", 0), ("x", 0), ("x", 1))


def swap(array, axis, bit):
    return lax.ppermute(array, axis, [(i, i ^ (1 << bit)) for i in range(lax.axis_size(axis))])


def dot_nt(a, b):
    return lax.dot_general(a, b, (((1,), (1,)), ((), ())), preferred_element_type=F32)


def dot_nn(a, b):
    return lax.dot_general(a, b, (((1,), (0,)), ((), ())), preferred_element_type=F32)


def total_of(stack):
    return lax.reduce_precision(jnp.sum(stack.astype(F32), axis=0), 8, 7).astype(BF16)


def fetch(src, dst, sem, lo, size):
    part = pl.ds(lo, size)
    return pltpu.make_async_copy(src.at[part], dst.at[part], sem)


def both(mine, other, lo, hi, at, size):
    return jnp.concatenate([ref[lo:hi, at : at + size] for ref in (mine, other)], axis=0)


def own_body(kinds, rows, rank, gathered, mine_in, other_in, out, tokens, mine, other, staged, sems):
    n = kinds * rows
    db = mine.shape[1]
    ways = ((mine_in, mine), (other_in, other))
    head = fetch(gathered, tokens, sems.at[0], 0, tokens.shape[0])
    right = [fetch(src, dst, sems.at[1 + i], 2 * n, rows) for i, (src, dst) in enumerate(ways)]
    up = [fetch(src, dst, sems.at[3 + i], 0, rows) for i, (src, dst) in enumerate(ways)]
    for copy in (head, *right, *up):
        copy.start()
    for copy in (head, *right, *up):
        copy.wait()
    part = dot_nt(tokens[:, db:], both(mine, other, 2 * n, 2 * n + rows, 0, rank))
    staged[...] = part + dot_nt(tokens[:, :db], both(mine, other, 0, rows, 0, db))
    store = pltpu.make_async_copy(staged, out, sems.at[5])
    store.start()
    store.wait()


def own_call(gathered, mine, other, kinds):
    count, width = gathered.shape
    rows = mine.shape[0] // (2 * kinds + 2)
    args = (gathered, mine, other)
    out = ((count, 2 * rows), F32)
    return pl.pallas_call(
        functools.partial(own_body, kinds, rows, width - mine.shape[1]),
        out_shape=jax.ShapeDtypeStruct(*out),
        in_specs=[pl.BlockSpec(memory_space=pl.ANY)] * 3,
        out_specs=pl.BlockSpec(memory_space=pl.ANY),
        scratch_shapes=[pltpu.VMEM(a.shape, BF16) for a in args]
        + [pltpu.VMEM(*out), pltpu.SemaphoreType.DMA((6,))],
        compiler_params=pltpu.CompilerParams(vmem_limit_bytes=FFN_MIB * 2**20),
        name="ffn_own",
    )(*args)


def ffn_body(kinds, rows, rank, *refs):
    n = kinds * rows
    count = kinds + 2
    ins, outs = refs[:count], refs[count : count + kinds + 1]
    bufs, stage = refs[count + kinds + 1 : 2 * count + kinds + 1], refs[2 * count + kinds + 1 : -2]
    sems, out_sems = refs[-2:]
    xs, (mine, other) = bufs[:kinds], bufs[kinds:]
    db = mine.shape[1]
    head = db - rank

    def part(i, sem, lo, size):
        return fetch(ins[i], bufs[i], sems.at[sem], lo, size)

    def stored(k):
        copy = pltpu.make_async_copy(stage[k], outs[k], out_sems.at[k])
        copy.start()
        return copy

    first = [part(0, 0, 0, xs[0].shape[0])]
    late = []
    for i in (kinds, kinds + 1):
        first.append(part(i, i, rows, n - rows))
        late.append(part(i, i + 2, 2 * n, 2 * rows))
        late.append(part(i, i + 4, n, n))
    partners = [part(i, i, 0, xs[i].shape[0]) for i in range(1, kinds)]
    for copy in first + partners + late:
        copy.start()
    for copy in first:
        copy.wait()

    pre = xs[0][...]
    for k in range(1, kinds):
        partners[k - 1].wait()
        pre = pre + dot_nt(xs[k][...], both(mine, other, k * rows, (k + 1) * rows, 0, db))
    hidden = (0.5 * pre * (1.0 + lax.erf(pre * (0.5**0.5)))).astype(BF16)
    for copy in late:
        copy.wait()
    back = stage[kinds]
    back[:, :head] = dot_nn(hidden, both(mine, other, 2 * n, 2 * n + rows, rank, head)).astype(BF16)
    back[:, head:] = dot_nn(hidden, both(mine, other, 2 * n + rows, 2 * n + 2 * rows, 0, rank - head)).astype(BF16)
    stores = [stored(kinds)]
    for k in range(kinds):
        lo = n + k * rows
        stage[k][...] = dot_nn(hidden, both(mine, other, lo, lo + rows, 0, db)).astype(outs[k].dtype)
        stores.append(stored(k))
    for copy in stores:
        copy.wait()


def ffn_call(own, pieces, mine, other, rank, kinds):
    count = own.shape[0]
    db = mine.shape[1]
    rows = mine.shape[0] // (2 * kinds + 2)
    args = (own, *pieces, mine, other)
    outs = [((count, db), F32)] + [((count, db), BF16)] * (kinds - 1) + [((count, rank), BF16)]
    return pl.pallas_call(
        functools.partial(ffn_body, kinds, rows, rank),
        out_shape=[pltpu.HBM(*a) for a in outs],
        in_specs=[pl.BlockSpec(memory_space=pl.ANY)] * len(args),
        scratch_shapes=[pltpu.VMEM(a.shape, a.dtype) for a in args]
        + [pltpu.VMEM(*a) for a in outs]
        + [pltpu.SemaphoreType.DMA((len(args) + 4,)), pltpu.SemaphoreType.DMA((len(outs),))],
        compiler_params=pltpu.CompilerParams(vmem_limit_bytes=FFN_MIB * 2**20),
        name="ffn",
    )(*args)


def pack_body(rank, up, down, right, left, out, sems):
    n, db = up.shape
    rows = right.shape[0]
    head = db - rank
    moves = (
        (up, out.at[pl.ds(0, n)]),
        (down, out.at[pl.ds(n, n)]),
        (right, out.at[pl.ds(2 * n, rows), pl.ds(0, rank)]),
        (left.at[:, pl.ds(0, head)], out.at[pl.ds(2 * n, rows), pl.ds(rank, head)]),
        (left.at[:, pl.ds(head, rank - head)], out.at[pl.ds(2 * n + rows, rows), pl.ds(0, rank - head)]),
    )
    copies = [pltpu.make_async_copy(src, dst, sems.at[i]) for i, (src, dst) in enumerate(moves)]
    for copy in copies:
        copy.start()
    for copy in copies:
        copy.wait()


def pack_call(up, down, right, left):
    (n, db), (rows, rank) = up.shape, right.shape
    return pl.pallas_call(
        functools.partial(pack_body, rank),
        out_shape=pltpu.HBM((2 * n + 2 * rows, db), BF16),
        in_specs=[pl.BlockSpec(memory_space=pl.ANY)] * 4,
        scratch_shapes=[pltpu.SemaphoreType.DMA((5,))],
        compiler_params=pltpu.CompilerParams(vmem_limit_bytes=60 * 2**20),
        name="pack",
    )(up, down, right, left)


def code_body(x, w, stack):
    part = dot_nn(x[...], w[...]).astype(BF16)
    for i in range(stack.shape[0]):
        stack[i] = part


def code_call(tokens, up_left, n):
    shape = jax.ShapeDtypeStruct((n, tokens.shape[0], up_left.shape[1]), BF16)
    return pl.pallas_call(code_body, out_shape=shape, name="code_part", compiler_params=pltpu.CompilerParams(vmem_limit_bytes=60 * 2**20))(tokens, up_left)


def per_device(tokens, up_weight, down_weight, up_left, up_right, down_left, down_right):
    nz, nf = lax.axis_size("z"), lax.axis_size(FEAT)
    count, db = tokens.shape
    rows, rank = up_right.shape[1:]
    kinds = up_weight.shape[2]
    up = up_weight[0].transpose(1, 0, 2).reshape(kinds * rows, db)
    down = down_weight[0].transpose(1, 0, 2).reshape(kinds * rows, db)

    packed = pack_call(up, down, up_right[0], down_left[0])
    stack = code_call(tokens, up_left, nf)
    stack = lax.all_to_all(stack, FEAT, 0, 0, tiled=True)
    other = swap(packed, "yl", 0)
    mine = jnp.concatenate([tokens, total_of(stack)], axis=1)
    gathered = lax.all_gather(mine, "z", axis=0, tiled=True)
    own = gathered[:, :db]
    pieces = []
    for axis, bit in LEVEL_AXES:
        pieces.append(swap(own, axis, bit))

    own_pre = own_call(gathered, packed, other, kinds)
    own_total, *terms, back = ffn_call(own_pre, pieces, packed, other, rank, kinds)
    sent = []
    for part, (axis, bit) in zip(terms, LEVEL_AXES):
        sent.append(swap(part, axis, bit))
    back = lax.all_to_all(back.reshape(nz, count, rank), "z", 0, 0, tiled=True)
    total = own_total
    for s in sent:
        total = total + s.astype(F32)
    total = total.astype(BF16)
    total = lax.all_to_all(total.reshape(nz, count, db), "z", 0, 0, tiled=True)
    back = total_of(back)
    back = lax.all_gather(back, FEAT, axis=0)
    back = total_of(back)
    total = jnp.sum(total.astype(F32), axis=0)
    return (total + dot_nn(back, down_right)).astype(BF16)


def solution(mesh):
    tok, feat = ("z", "yl"), FEAT
    inner = Mesh(mesh.devices.reshape(16, 2, 4, 2, 2), tok + feat)
    return jax.shard_map(
        per_device,
        mesh=inner,
        in_specs=(
            P(tok, feat),
            P(feat, tok, None, None),
            P(feat, tok, None, None),
            P(feat, None),
            P(feat, tok, None),
            P(feat, tok, None),
            P(None, feat),
        ),
        out_specs=P(tok, feat),
        check_vma=False,
    )
```

```python
import functools

import jax
import jax.numpy as jnp
from jax import lax
from jax.experimental import pallas as pl
from jax.experimental.pallas import tpu as pltpu
from jax.sharding import Mesh, PartitionSpec as P


F32 = jnp.float32
BF16 = jnp.bfloat16
FEAT = ("x", "yh", "c")
FFN_MIB = 24
LEVEL_AXES = (("c", 0), ("yh", 0), ("x", 0), ("x", 1))


def swap(array, axis, bit):
    return lax.ppermute(array, axis, [(i, i ^ (1 << bit)) for i in range(lax.axis_size(axis))])


def dot_nt(a, b):
    return lax.dot_general(a, b, (((1,), (1,)), ((), ())), preferred_element_type=F32)


def dot_nn(a, b):
    return lax.dot_general(a, b, (((1,), (0,)), ((), ())), preferred_element_type=F32)


def share(array, axis):
    n = lax.axis_size(axis)
    return lax.all_to_all(jnp.broadcast_to(array[None], (n,) + array.shape), axis, 0, 0, tiled=True)


def total_of(stack):
    return lax.reduce_precision(jnp.sum(stack.astype(F32), axis=0), 8, 7).astype(BF16)


def fetch(src, dst, sem, lo, size):
    part = pl.ds(lo, size)
    return pltpu.make_async_copy(src.at[part], dst.at[part], sem)


def ffn_body(kinds, rows, rank, *refs):
    n = kinds * rows
    count = kinds + 3
    ins, outs = refs[:count], refs[count : count + kinds + 1]
    bufs, stage = refs[count + kinds + 1 : 2 * count + kinds + 1], refs[2 * count + kinds + 1 : -2]
    sems, out_sems = refs[-2:]
    xs, (code, mine, other) = bufs[:kinds], bufs[kinds:]
    db = mine.shape[1]
    head = db - rank

    def part(i, sem, lo, size):
        return fetch(ins[i], bufs[i], sems.at[sem], lo, size)

    def stored(k):
        copy = pltpu.make_async_copy(stage[k], outs[k], out_sems.at[k])
        copy.start()
        return copy

    first = [part(0, 0, 0, xs[0].shape[0])]
    late = []
    for i in (kinds + 1, kinds + 2):
        first.append(part(i, i, 0, n))
        late.append(part(i, i + 2, 2 * n, 2 * rows))
        late.append(part(i, i + 4, n, n))
    partners = [part(i, i, 0, xs[i].shape[0]) for i in range(1, kinds)]
    last = part(kinds, kinds, 0, code.shape[0])
    for copy in (*first, *partners, *late, last):
        copy.start()
    for copy in first:
        copy.wait()

    def both(lo, hi, at, size):
        return jnp.concatenate([ref[lo:hi, at : at + size] for ref in (mine, other)], axis=0)

    pre = dot_nt(xs[0][...], both(0, rows, 0, db))
    for k in range(1, kinds):
        partners[k - 1].wait()
        pre = pre + dot_nt(xs[k][...], both(k * rows, (k + 1) * rows, 0, db))
    for copy in (*late, last):
        copy.wait()
    pre = pre + dot_nt(code[...], both(2 * n, 2 * n + rows, 0, rank))
    hidden = (0.5 * pre * (1.0 + lax.erf(pre * (0.5**0.5)))).astype(BF16)
    back = stage[kinds]
    back[:, :head] = dot_nn(hidden, both(2 * n, 2 * n + rows, rank, head)).astype(BF16)
    back[:, head:] = dot_nn(hidden, both(2 * n + rows, 2 * n + 2 * rows, 0, rank - head)).astype(BF16)
    stores = [stored(kinds)]
    for k in range(kinds):
        lo = n + k * rows
        stage[k][...] = dot_nn(hidden, both(lo, lo + rows, 0, db)).astype(outs[k].dtype)
        stores.append(stored(k))
    for copy in stores:
        copy.wait()


def ffn_call(pieces, code, mine, other):
    count, rank = code.shape
    db, kinds = mine.shape[1], len(pieces)
    rows = mine.shape[0] // (2 * kinds + 2)
    args = (*pieces, code, mine, other)
    outs = [((count, db), F32)] + [((count, db), BF16)] * (kinds - 1) + [((count, rank), BF16)]
    return pl.pallas_call(
        functools.partial(ffn_body, kinds, rows, rank),
        out_shape=[pltpu.HBM(*a) for a in outs],
        in_specs=[pl.BlockSpec(memory_space=pl.ANY)] * len(args),
        scratch_shapes=[pltpu.VMEM(a.shape, BF16) for a in args]
        + [pltpu.VMEM(*a) for a in outs]
        + [pltpu.SemaphoreType.DMA((len(args) + 4,)), pltpu.SemaphoreType.DMA((len(outs),))],
        compiler_params=pltpu.CompilerParams(vmem_limit_bytes=FFN_MIB * 2**20),
        name="ffn",
    )(*args)


def pack_body(rank, up, down, right, left, out, sems):
    n, db = up.shape
    rows = right.shape[0]
    head = db - rank
    moves = (
        (up, out.at[pl.ds(0, n)]),
        (down, out.at[pl.ds(n, n)]),
        (right, out.at[pl.ds(2 * n, rows), pl.ds(0, rank)]),
        (left.at[:, pl.ds(0, head)], out.at[pl.ds(2 * n, rows), pl.ds(rank, head)]),
        (left.at[:, pl.ds(head, rank - head)], out.at[pl.ds(2 * n + rows, rows), pl.ds(0, rank - head)]),
    )
    copies = [pltpu.make_async_copy(src, dst, sems.at[i]) for i, (src, dst) in enumerate(moves)]
    for copy in copies:
        copy.start()
    for copy in copies:
        copy.wait()


def pack_call(up, down, right, left):
    (n, db), (rows, rank) = up.shape, right.shape
    return pl.pallas_call(
        functools.partial(pack_body, rank),
        out_shape=pltpu.HBM((2 * n + 2 * rows, db), BF16),
        in_specs=[pl.BlockSpec(memory_space=pl.ANY)] * 4,
        scratch_shapes=[pltpu.SemaphoreType.DMA((5,))],
        compiler_params=pltpu.CompilerParams(vmem_limit_bytes=60 * 2**20),
        name="pack",
    )(up, down, right, left)


def per_device(tokens, up_weight, down_weight, up_left, up_right, down_left, down_right):
    nz, nf = lax.axis_size("z"), lax.axis_size(FEAT)
    count, db = tokens.shape
    rows, rank = up_right.shape[1:]
    kinds = up_weight.shape[2]
    up = up_weight[0].transpose(1, 0, 2).reshape(kinds * rows, db)
    down = down_weight[0].transpose(1, 0, 2).reshape(kinds * rows, db)

    own = lax.all_to_all(jnp.broadcast_to(tokens[None], (nz, count, db)), "z", 0, 0, tiled=True)
    own = own.reshape(nz * count, db)
    packed = pack_call(up, down, up_right[0], down_left[0])
    other = swap(packed, "yl", 0)
    part = dot_nn(own, up_left).astype(BF16)
    part = lax.all_to_all(part.reshape(nf, nz * count // nf, rank), FEAT, 0, 0, tiled=True)
    group = total_of(part)
    code = share(group, FEAT).reshape(nz * count, rank)
    pieces = [own]
    for axis, bit in LEVEL_AXES:
        pieces.append(swap(own, axis, bit))
    own_total, *terms, back = ffn_call(pieces, code, packed, other)
    sent = []
    for part, (axis, bit) in zip(terms, LEVEL_AXES):
        sent.append(swap(part, axis, bit))
    back = lax.all_to_all(back.reshape(nz, count, rank), "z", 0, 0, tiled=True)
    total = own_total
    for s in sent:
        total = total + s.astype(F32)
    total = total.astype(BF16)
    total = lax.all_to_all(total.reshape(nz, count, db), "z", 0, 0, tiled=True)
    back = total_of(back)
    back = lax.all_gather(back, FEAT, axis=0)
    back = total_of(back)
    total = jnp.sum(total.astype(F32), axis=0)
    return (total + dot_nn(back, down_right)).astype(BF16)


def solution(mesh):
    tok, feat = ("z", "yl"), FEAT
    inner = Mesh(mesh.devices.reshape(16, 2, 4, 2, 2), tok + feat)
    return jax.shard_map(
        per_device,
        mesh=inner,
        in_specs=(
            P(tok, feat),
            P(feat, tok, None, None),
            P(feat, tok, None, None),
            P(feat, None),
            P(feat, tok, None),
            P(feat, tok, None),
            P(None, feat),
        ),
        out_specs=P(tok, feat),
        check_vma=False,
    )
```

```python
import functools

import jax
import jax.numpy as jnp
from jax import lax
from jax.experimental import pallas as pl
from jax.experimental.pallas import tpu as pltpu
from jax.sharding import Mesh, PartitionSpec as P


F32 = jnp.float32
BF16 = jnp.bfloat16
FEAT = ("x", "yh", "c")
FFN_MIB = 24
LEVEL_AXES = (("c", 0), ("yh", 0), ("x", 0), ("x", 1))


def swap(array, axis, bit):
    return lax.ppermute(array, axis, [(i, i ^ (1 << bit)) for i in range(lax.axis_size(axis))])


def dot_nt(a, b):
    return lax.dot_general(a, b, (((1,), (1,)), ((), ())), preferred_element_type=F32)


def dot_nn(a, b):
    return lax.dot_general(a, b, (((1,), (0,)), ((), ())), preferred_element_type=F32)


def total_of(stack):
    return lax.reduce_precision(jnp.sum(stack.astype(F32), axis=0), 8, 7).astype(BF16)


def ffn_body(kinds, rows, rank, *refs):
    n = kinds * rows
    count = kinds + 2
    xs, (mine, other_in), outs = refs[:kinds], refs[kinds:count], refs[count : count + kinds + 1]
    stage, (other, sems, out_sems) = refs[count + kinds + 1 : -3], refs[-3:]
    db = mine.shape[1]
    head = db - rank

    def fetch(sem, lo, size):
        rows_of = pl.ds(lo, size)
        copy = pltpu.make_async_copy(other_in.at[rows_of], other.at[rows_of], sems.at[sem])
        copy.start()
        return copy

    def stored(k):
        copy = pltpu.make_async_copy(stage[k], outs[k], out_sems.at[k])
        copy.start()
        return copy

    def both(lo, hi, at, size):
        return jnp.concatenate([ref[lo:hi, at : at + size] for ref in (mine, other)], axis=0)

    low_rank, ups, downs = fetch(0, 2 * n, 2 * rows), fetch(1, 0, n), fetch(2, n, n)
    low_rank.wait()
    pre = dot_nt(xs[0][:, db:], both(2 * n, 2 * n + rows, 0, rank))
    ups.wait()
    pre = pre + dot_nt(xs[0][:, :db], both(0, rows, 0, db))
    for k in range(1, kinds):
        pre = pre + dot_nt(xs[k][...], both(k * rows, (k + 1) * rows, 0, db))
    hidden = (0.5 * pre * (1.0 + lax.erf(pre * (0.5**0.5)))).astype(BF16)
    back = stage[kinds]
    back[:, :head] = dot_nn(hidden, both(2 * n, 2 * n + rows, rank, head)).astype(BF16)
    back[:, head:] = dot_nn(hidden, both(2 * n + rows, 2 * n + 2 * rows, 0, rank - head)).astype(BF16)
    stores = [stored(kinds)]
    downs.wait()
    for k in range(kinds):
        lo = n + k * rows
        stage[k][...] = dot_nn(hidden, both(lo, lo + rows, 0, db)).astype(outs[k].dtype)
        stores.append(stored(k))
    for copy in stores:
        copy.wait()


def ffn_call(gathered, pieces, mine, other, kinds):
    count, width = gathered.shape
    db = mine.shape[1]
    rank = width - db
    rows = mine.shape[0] // (2 * kinds + 2)
    args = (gathered, *pieces, mine, other)
    outs = [((count, db), F32)] + [((count, db), BF16)] * (kinds - 1) + [((count, rank), BF16)]
    return pl.pallas_call(
        functools.partial(ffn_body, kinds, rows, rank),
        out_shape=[pltpu.HBM(*a) for a in outs],
        out_specs=[pl.BlockSpec(memory_space=pl.ANY)] * len(outs),
        in_specs=[pl.BlockSpec(memory_space=pltpu.VMEM)] * (len(args) - 1) + [pl.BlockSpec(memory_space=pl.ANY)],
        scratch_shapes=[pltpu.VMEM(*a) for a in outs]
        + [pltpu.VMEM(other.shape, BF16), pltpu.SemaphoreType.DMA((3,)), pltpu.SemaphoreType.DMA((len(outs),))],
        compiler_params=pltpu.CompilerParams(vmem_limit_bytes=FFN_MIB * 2**20),
        name="ffn",
    )(*args)


def pack_body(rank, up, down, right, left, out, sems):
    n, db = up.shape
    rows = right.shape[0]
    head = db - rank
    moves = (
        (up, out.at[pl.ds(0, n)]),
        (down, out.at[pl.ds(n, n)]),
        (right, out.at[pl.ds(2 * n, rows), pl.ds(0, rank)]),
        (left.at[:, pl.ds(0, head)], out.at[pl.ds(2 * n, rows), pl.ds(rank, head)]),
        (left.at[:, pl.ds(head, rank - head)], out.at[pl.ds(2 * n + rows, rows), pl.ds(0, rank - head)]),
    )
    copies = [pltpu.make_async_copy(src, dst, sems.at[i]) for i, (src, dst) in enumerate(moves)]
    for copy in copies:
        copy.start()
    for copy in copies:
        copy.wait()


def pack_call(up, down, right, left):
    (n, db), (rows, rank) = up.shape, right.shape
    return pl.pallas_call(
        functools.partial(pack_body, rank),
        out_shape=pltpu.HBM((2 * n + 2 * rows, db), BF16),
        in_specs=[pl.BlockSpec(memory_space=pl.ANY)] * 4,
        scratch_shapes=[pltpu.SemaphoreType.DMA((5,))],
        compiler_params=pltpu.CompilerParams(vmem_limit_bytes=60 * 2**20),
        name="pack",
    )(up, down, right, left)


def code_body(x, w, stack):
    part = dot_nn(x[...], w[...]).astype(BF16)
    for i in range(stack.shape[0]):
        stack[i] = part


def code_call(tokens, up_left, n):
    shape = jax.ShapeDtypeStruct((n, tokens.shape[0], up_left.shape[1]), BF16)
    return pl.pallas_call(code_body, out_shape=shape, name="code_part", compiler_params=pltpu.CompilerParams(vmem_limit_bytes=60 * 2**20))(tokens, up_left)


def per_device(tokens, up_weight, down_weight, up_left, up_right, down_left, down_right):
    nz, nf = lax.axis_size("z"), lax.axis_size(FEAT)
    count, db = tokens.shape
    rows, rank = up_right.shape[1:]
    kinds = up_weight.shape[2]
    up = up_weight[0].transpose(1, 0, 2).reshape(kinds * rows, db)
    down = down_weight[0].transpose(1, 0, 2).reshape(kinds * rows, db)

    packed = pack_call(up, down, up_right[0], down_left[0])
    stack = code_call(tokens, up_left, nf)
    stack = lax.all_to_all(stack, FEAT, 0, 0, tiled=True)
    other = swap(packed, "yl", 0)
    mine = jnp.concatenate([tokens, total_of(stack)], axis=1)
    gathered = lax.all_gather(mine, "z", axis=0, tiled=True)
    own = gathered[:, :db]
    pieces = []
    for axis, bit in LEVEL_AXES:
        pieces.append(swap(own, axis, bit))

    own_total, *terms, back = ffn_call(gathered, pieces, packed, other, kinds)
    sent = []
    for part, (axis, bit) in zip(terms, LEVEL_AXES):
        sent.append(swap(part, axis, bit))
    back = lax.all_to_all(back.reshape(nz, count, rank), "z", 0, 0, tiled=True)
    total = own_total
    for s in sent:
        total = total + s.astype(F32)
    total = total.astype(BF16)
    total = lax.all_to_all(total.reshape(nz, count, db), "z", 0, 0, tiled=True)
    back = total_of(back)
    back = lax.all_gather(back, FEAT, axis=0)
    back = total_of(back)
    total = jnp.sum(total.astype(F32), axis=0)
    return (total + dot_nn(back, down_right)).astype(BF16)


def solution(mesh):
    tok, feat = ("z", "yl"), FEAT
    inner = Mesh(mesh.devices.reshape(16, 2, 4, 2, 2), tok + feat)
    return jax.shard_map(
        per_device,
        mesh=inner,
        in_specs=(
            P(tok, feat),
            P(feat, tok, None, None),
            P(feat, tok, None, None),
            P(feat, None),
            P(feat, tok, None),
            P(feat, tok, None),
            P(None, feat),
        ),
        out_specs=P(tok, feat),
        check_vma=False,
    )
```

```python
import functools

import jax
import jax.numpy as jnp
from jax import lax
from jax.experimental import pallas as pl
from jax.experimental.pallas import tpu as pltpu
from jax.sharding import Mesh, PartitionSpec as P


F32 = jnp.float32
BF16 = jnp.bfloat16
FEAT = ("x", "yh", "c")
FFN_MIB = 24
LEVEL_AXES = (("c", 0), ("yh", 0), ("x", 0), ("x", 1))


def swap(array, axis, bit):
    return lax.ppermute(array, axis, [(i, i ^ (1 << bit)) for i in range(lax.axis_size(axis))])


def dot_nt(a, b):
    return lax.dot_general(a, b, (((1,), (1,)), ((), ())), preferred_element_type=F32)


def dot_nn(a, b):
    return lax.dot_general(a, b, (((1,), (0,)), ((), ())), preferred_element_type=F32)


def total_of(stack):
    return lax.reduce_precision(jnp.sum(stack.astype(F32), axis=0), 8, 7).astype(BF16)


def both(mine, other, lo, hi, at, size):
    return jnp.concatenate([ref[lo:hi, at : at + size] for ref in (mine, other)], axis=0)


def own_body(n, rank, gathered, mine, other_in, out, other, sems):
    rows, db = other.shape[0] // 2, other.shape[1]
    right = pltpu.make_async_copy(other_in.at[pl.ds(2 * n, rows)], other.at[pl.ds(0, rows)], sems.at[0])
    up = pltpu.make_async_copy(other_in.at[pl.ds(0, rows)], other.at[pl.ds(rows, rows)], sems.at[1])
    right.start()
    up.start()
    right.wait()
    weight = jnp.concatenate([mine[2 * n : 2 * n + rows, :rank], other[:rows, :rank]], axis=0)
    part = dot_nt(gathered[:, db:], weight)
    up.wait()
    out[...] = part + dot_nt(gathered[:, :db], jnp.concatenate([mine[:rows, :], other[rows:, :]], axis=0))


def own_call(gathered, mine, other, kinds):
    count, width = gathered.shape
    db = mine.shape[1]
    rows = mine.shape[0] // (2 * kinds + 2)
    vmem = pl.BlockSpec(memory_space=pltpu.VMEM)
    return pl.pallas_call(
        functools.partial(own_body, kinds * rows, width - db),
        out_shape=jax.ShapeDtypeStruct((count, 2 * rows), F32),
        in_specs=[vmem, vmem, pl.BlockSpec(memory_space=pl.ANY)],
        scratch_shapes=[pltpu.VMEM((2 * rows, db), BF16), pltpu.SemaphoreType.DMA((2,))],
        compiler_params=pltpu.CompilerParams(vmem_limit_bytes=FFN_MIB * 2**20),
        name="ffn_own",
    )(gathered, mine, other)


def ffn_body(kinds, rows, rank, *refs):
    n = kinds * rows
    count = kinds + 2
    xs, (mine, other_in), outs = refs[:kinds], refs[kinds:count], refs[count : count + kinds + 1]
    stage, (other, sems, out_sems) = refs[count + kinds + 1 : -3], refs[-3:]
    db = mine.shape[1]
    head = db - rank

    def fetch(sem, lo, size):
        rows_of = pl.ds(lo, size)
        copy = pltpu.make_async_copy(other_in.at[rows_of], other.at[rows_of], sems.at[sem])
        copy.start()
        return copy

    def stored(k):
        copy = pltpu.make_async_copy(stage[k], outs[k], out_sems.at[k])
        copy.start()
        return copy

    ups, low_rank, downs = fetch(1, rows, n - rows), fetch(0, 2 * n, 2 * rows), fetch(2, n, n)
    pre = xs[0][...]
    ups.wait()
    for k in range(1, kinds):
        pre = pre + dot_nt(xs[k][...], both(mine, other, k * rows, (k + 1) * rows, 0, db))
    hidden = (0.5 * pre * (1.0 + lax.erf(pre * (0.5**0.5)))).astype(BF16)
    low_rank.wait()
    back = stage[kinds]
    back[:, :head] = dot_nn(hidden, both(mine, other, 2 * n, 2 * n + rows, rank, head)).astype(BF16)
    back[:, head:] = dot_nn(hidden, both(mine, other, 2 * n + rows, 2 * n + 2 * rows, 0, rank - head)).astype(BF16)
    stores = [stored(kinds)]
    downs.wait()
    for k in range(kinds):
        lo = n + k * rows
        stage[k][...] = dot_nn(hidden, both(mine, other, lo, lo + rows, 0, db)).astype(outs[k].dtype)
        stores.append(stored(k))
    for copy in stores:
        copy.wait()


def ffn_call(own, pieces, mine, other, rank, kinds):
    count, db = own.shape[0], mine.shape[1]
    rows = mine.shape[0] // (2 * kinds + 2)
    args = (own, *pieces, mine, other)
    outs = [((count, db), F32)] + [((count, db), BF16)] * (kinds - 1) + [((count, rank), BF16)]
    return pl.pallas_call(
        functools.partial(ffn_body, kinds, rows, rank),
        out_shape=[pltpu.HBM(*a) for a in outs],
        out_specs=[pl.BlockSpec(memory_space=pl.ANY)] * len(outs),
        in_specs=[pl.BlockSpec(memory_space=pltpu.VMEM)] * (len(args) - 1) + [pl.BlockSpec(memory_space=pl.ANY)],
        scratch_shapes=[pltpu.VMEM(*a) for a in outs]
        + [pltpu.VMEM(other.shape, BF16), pltpu.SemaphoreType.DMA((3,)), pltpu.SemaphoreType.DMA((len(outs),))],
        compiler_params=pltpu.CompilerParams(vmem_limit_bytes=FFN_MIB * 2**20),
        name="ffn",
    )(*args)


def pack_body(rank, up, down, right, left, out, sems):
    n, db = up.shape
    rows = right.shape[0]
    head = db - rank
    moves = (
        (up, out.at[pl.ds(0, n)]),
        (down, out.at[pl.ds(n, n)]),
        (right, out.at[pl.ds(2 * n, rows), pl.ds(0, rank)]),
        (left.at[:, pl.ds(0, head)], out.at[pl.ds(2 * n, rows), pl.ds(rank, head)]),
        (left.at[:, pl.ds(head, rank - head)], out.at[pl.ds(2 * n + rows, rows), pl.ds(0, rank - head)]),
    )
    copies = [pltpu.make_async_copy(src, dst, sems.at[i]) for i, (src, dst) in enumerate(moves)]
    for copy in copies:
        copy.start()
    for copy in copies:
        copy.wait()


def pack_call(up, down, right, left):
    (n, db), (rows, rank) = up.shape, right.shape
    return pl.pallas_call(
        functools.partial(pack_body, rank),
        out_shape=pltpu.HBM((2 * n + 2 * rows, db), BF16),
        in_specs=[pl.BlockSpec(memory_space=pl.ANY)] * 4,
        scratch_shapes=[pltpu.SemaphoreType.DMA((5,))],
        compiler_params=pltpu.CompilerParams(vmem_limit_bytes=60 * 2**20),
        name="pack",
    )(up, down, right, left)


def code_body(x, w, stack):
    part = dot_nn(x[...], w[...]).astype(BF16)
    for i in range(stack.shape[0]):
        stack[i] = part


def code_call(tokens, up_left, n):
    shape = jax.ShapeDtypeStruct((n, tokens.shape[0], up_left.shape[1]), BF16)
    return pl.pallas_call(code_body, out_shape=shape, name="code_part", compiler_params=pltpu.CompilerParams(vmem_limit_bytes=60 * 2**20))(tokens, up_left)


def per_device(tokens, up_weight, down_weight, up_left, up_right, down_left, down_right):
    nz, nf = lax.axis_size("z"), lax.axis_size(FEAT)
    count, db = tokens.shape
    rows, rank = up_right.shape[1:]
    kinds = up_weight.shape[2]
    up = up_weight[0].transpose(1, 0, 2).reshape(kinds * rows, db)
    down = down_weight[0].transpose(1, 0, 2).reshape(kinds * rows, db)

    packed = pack_call(up, down, up_right[0], down_left[0])
    stack = code_call(tokens, up_left, nf)
    stack = lax.all_to_all(stack, FEAT, 0, 0, tiled=True)
    other = swap(packed, "yl", 0)
    mine = jnp.concatenate([tokens, total_of(stack)], axis=1)
    gathered = lax.all_gather(mine, "z", axis=0, tiled=True)
    own = gathered[:, :db]
    pieces = []
    for axis, bit in LEVEL_AXES:
        pieces.append(swap(own, axis, bit))

    own_pre = own_call(gathered, packed, other, kinds)
    own_total, *terms, back = ffn_call(own_pre, pieces, packed, other, rank, kinds)
    sent = []
    for part, (axis, bit) in zip(terms, LEVEL_AXES):
        sent.append(swap(part, axis, bit))
    back = lax.all_to_all(back.reshape(nz, count, rank), "z", 0, 0, tiled=True)
    total = own_total
    for s in sent:
        total = total + s.astype(F32)
    total = total.astype(BF16)
    total = lax.all_to_all(total.reshape(nz, count, db), "z", 0, 0, tiled=True)
    back = total_of(back)
    back = lax.all_gather(back, FEAT, axis=0)
    back = total_of(back)
    total = jnp.sum(total.astype(F32), axis=0)
    return (total + dot_nn(back, down_right)).astype(BF16)


def solution(mesh):
    tok, feat = ("z", "yl"), FEAT
    inner = Mesh(mesh.devices.reshape(16, 2, 4, 2, 2), tok + feat)
    return jax.shard_map(
        per_device,
        mesh=inner,
        in_specs=(
            P(tok, feat),
            P(feat, tok, None, None),
            P(feat, tok, None, None),
            P(feat, None),
            P(feat, tok, None),
            P(feat, tok, None),
            P(None, feat),
        ),
        out_specs=P(tok, feat),
        check_vma=False,
    )
```

```python
import functools

import jax
import jax.numpy as jnp
from jax import lax
from jax.experimental import pallas as pl
from jax.experimental.pallas import tpu as pltpu
from jax.sharding import Mesh, PartitionSpec as P


F32 = jnp.float32
BF16 = jnp.bfloat16
FEAT = ("x", "yh", "c")
FFN_MIB = 24
LEVEL_AXES = (("c", 0), ("yh", 0), ("x", 0), ("x", 1))


def swap(array, axis, bit):
    return lax.ppermute(array, axis, [(i, i ^ (1 << bit)) for i in range(lax.axis_size(axis))])


def dot_nt(a, b):
    return lax.dot_general(a, b, (((1,), (1,)), ((), ())), preferred_element_type=F32)


def dot_nn(a, b):
    return lax.dot_general(a, b, (((1,), (0,)), ((), ())), preferred_element_type=F32)


def total_of(stack):
    return lax.reduce_precision(jnp.sum(stack.astype(F32), axis=0), 8, 7).astype(BF16)


def both(mine, other, lo, hi, at, size):
    return jnp.concatenate([ref[lo:hi, at : at + size] for ref in (mine, other)], axis=0)


def own_body(n, rank, gathered, mine, other_in, out, other, sems):
    rows, db = other.shape[0] // 2, other.shape[1]
    right = pltpu.make_async_copy(other_in.at[pl.ds(2 * n, rows)], other.at[pl.ds(0, rows)], sems.at[0])
    up = pltpu.make_async_copy(other_in.at[pl.ds(0, rows)], other.at[pl.ds(rows, rows)], sems.at[1])
    right.start()
    up.start()
    right.wait()
    weight = jnp.concatenate([mine[2 * n : 2 * n + rows, :rank], other[:rows, :rank]], axis=0)
    part = dot_nt(gathered[:, db:], weight)
    up.wait()
    out[...] = part + dot_nt(gathered[:, :db], jnp.concatenate([mine[:rows, :], other[rows:, :]], axis=0))


def own_call(gathered, mine, other, kinds):
    count, width = gathered.shape
    db = mine.shape[1]
    rows = mine.shape[0] // (2 * kinds + 2)
    vmem = pl.BlockSpec(memory_space=pltpu.VMEM)
    return pl.pallas_call(
        functools.partial(own_body, kinds * rows, width - db),
        out_shape=jax.ShapeDtypeStruct((count, 2 * rows), F32),
        in_specs=[vmem, vmem, pl.BlockSpec(memory_space=pl.ANY)],
        scratch_shapes=[pltpu.VMEM((2 * rows, db), BF16), pltpu.SemaphoreType.DMA((2,))],
        compiler_params=pltpu.CompilerParams(vmem_limit_bytes=FFN_MIB * 2**20),
        name="ffn_own",
    )(gathered, mine, other)


def ffn_body(kinds, rows, rank, *refs):
    n = kinds * rows
    count = kinds + 2
    xs, (mine, other_in), outs = refs[:kinds], refs[kinds:count], refs[count : count + kinds + 1]
    stage, (other, sems, out_sems) = refs[count + kinds + 1 : -3], refs[-3:]
    db = mine.shape[1]
    head = db - rank

    def fetch(sem, lo, size):
        rows_of = pl.ds(lo, size)
        copy = pltpu.make_async_copy(other_in.at[rows_of], other.at[rows_of], sems.at[sem])
        copy.start()
        return copy

    def stored(k):
        copy = pltpu.make_async_copy(stage[k], outs[k], out_sems.at[k])
        copy.start()
        return copy

    ups, low_rank, downs = fetch(1, rows, n - rows), fetch(0, 2 * n, 2 * rows), fetch(2, n, n)
    pre = xs[0][...]
    ups.wait()
    for k in range(1, kinds):
        pre = pre + dot_nt(xs[k][...], both(mine, other, k * rows, (k + 1) * rows, 0, db))
    hidden = (0.5 * pre * (1.0 + lax.erf(pre * (0.5**0.5)))).astype(BF16)
    low_rank.wait()
    back = stage[kinds]
    back[:, :head] = dot_nn(hidden, both(mine, other, 2 * n, 2 * n + rows, rank, head)).astype(BF16)
    back[:, head:] = dot_nn(hidden, both(mine, other, 2 * n + rows, 2 * n + 2 * rows, 0, rank - head)).astype(BF16)
    stores = [stored(kinds)]
    downs.wait()
    for k in range(kinds):
        lo = n + k * rows
        stage[k][...] = dot_nn(hidden, both(mine, other, lo, lo + rows, 0, db)).astype(outs[k].dtype)
        stores.append(stored(k))
    for copy in stores:
        copy.wait()


def ffn_call(own, pieces, mine, other, rank, kinds):
    count, db = own.shape[0], mine.shape[1]
    rows = mine.shape[0] // (2 * kinds + 2)
    args = (own, *pieces, mine, other)
    outs = [((count, db), F32)] + [((count, db), BF16)] * (kinds - 1) + [((count, rank), BF16)]
    return pl.pallas_call(
        functools.partial(ffn_body, kinds, rows, rank),
        out_shape=[pltpu.HBM(*a) for a in outs],
        out_specs=[pl.BlockSpec(memory_space=pl.ANY)] * len(outs),
        in_specs=[pl.BlockSpec(memory_space=pltpu.VMEM)] * (len(args) - 1) + [pl.BlockSpec(memory_space=pl.ANY)],
        scratch_shapes=[pltpu.VMEM(*a) for a in outs]
        + [pltpu.VMEM(other.shape, BF16), pltpu.SemaphoreType.DMA((3,)), pltpu.SemaphoreType.DMA((len(outs),))],
        compiler_params=pltpu.CompilerParams(vmem_limit_bytes=FFN_MIB * 2**20),
        name="ffn",
    )(*args)


def pack_body(rank, up, down, right, left, out, sems):
    n, db = up.shape
    rows = right.shape[0]
    head = db - rank
    moves = (
        (up, out.at[pl.ds(0, n)]),
        (down, out.at[pl.ds(n, n)]),
        (right, out.at[pl.ds(2 * n, rows), pl.ds(0, rank)]),
        (left.at[:, pl.ds(0, head)], out.at[pl.ds(2 * n, rows), pl.ds(rank, head)]),
        (left.at[:, pl.ds(head, rank - head)], out.at[pl.ds(2 * n + rows, rows), pl.ds(0, rank - head)]),
    )
    copies = [pltpu.make_async_copy(src, dst, sems.at[i]) for i, (src, dst) in enumerate(moves)]
    for copy in copies:
        copy.start()
    for copy in copies:
        copy.wait()


def pack_call(up, down, right, left):
    (n, db), (rows, rank) = up.shape, right.shape
    return pl.pallas_call(
        functools.partial(pack_body, rank),
        out_shape=pltpu.HBM((2 * n + 2 * rows, db), BF16),
        in_specs=[pl.BlockSpec(memory_space=pl.ANY)] * 4,
        scratch_shapes=[pltpu.SemaphoreType.DMA((5,))],
        compiler_params=pltpu.CompilerParams(vmem_limit_bytes=60 * 2**20),
        name="pack",
    )(up, down, right, left)


def code_body(chunks, x, w_in, stack, w, part, sems, out_sems):
    size = w.shape[0] // chunks
    loads = []
    for i in range(chunks):
        piece = pl.ds(i * size, size)
        loads.append(pltpu.make_async_copy(w_in.at[piece], w.at[piece], sems.at[i]))
        loads[i].start()
    total = jnp.zeros(part.shape, F32)
    for i in range(chunks):
        loads[i].wait()
        total = total + dot_nn(x[:, i * size : (i + 1) * size], w[i * size : (i + 1) * size, :])
    part[...] = total.astype(BF16)
    stores = [pltpu.make_async_copy(part, stack.at[i], out_sems.at[i]) for i in range(stack.shape[0])]
    for copy in stores:
        copy.start()
    for copy in stores:
        copy.wait()


def code_call(tokens, up_left, n):
    count, rank = tokens.shape[0], up_left.shape[1]
    chunks = 3
    return pl.pallas_call(
        functools.partial(code_body, chunks),
        out_shape=pltpu.HBM((n, count, rank), BF16),
        in_specs=[pl.BlockSpec(memory_space=pltpu.VMEM), pl.BlockSpec(memory_space=pl.ANY)],
        out_specs=pl.BlockSpec(memory_space=pl.ANY),
        scratch_shapes=[
            pltpu.VMEM(up_left.shape, BF16),
            pltpu.VMEM((count, rank), BF16),
            pltpu.SemaphoreType.DMA((chunks,)),
            pltpu.SemaphoreType.DMA((n,)),
        ],
        name="code_part",
        compiler_params=pltpu.CompilerParams(vmem_limit_bytes=60 * 2**20),
    )(tokens, up_left)


def per_device(tokens, up_weight, down_weight, up_left, up_right, down_left, down_right):
    nz, nf = lax.axis_size("z"), lax.axis_size(FEAT)
    count, db = tokens.shape
    rows, rank = up_right.shape[1:]
    kinds = up_weight.shape[2]
    up = up_weight[0].transpose(1, 0, 2).reshape(kinds * rows, db)
    down = down_weight[0].transpose(1, 0, 2).reshape(kinds * rows, db)

    packed = pack_call(up, down, up_right[0], down_left[0])
    stack = code_call(tokens, up_left, nf)
    stack = lax.all_to_all(stack, FEAT, 0, 0, tiled=True)
    other = swap(packed, "yl", 0)
    mine = jnp.concatenate([tokens, total_of(stack)], axis=1)
    gathered = lax.all_gather(mine, "z", axis=0, tiled=True)
    own = gathered[:, :db]
    pieces = []
    for axis, bit in LEVEL_AXES:
        pieces.append(swap(own, axis, bit))

    own_pre = own_call(gathered, packed, other, kinds)
    own_total, *terms, back = ffn_call(own_pre, pieces, packed, other, rank, kinds)
    sent = []
    for part, (axis, bit) in zip(terms, LEVEL_AXES):
        sent.append(swap(part, axis, bit))
    back = lax.all_to_all(back.reshape(nz, count, rank), "z", 0, 0, tiled=True)
    total = own_total
    for s in sent:
        total = total + s.astype(F32)
    total = total.astype(BF16)
    total = lax.all_to_all(total.reshape(nz, count, db), "z", 0, 0, tiled=True)
    back = total_of(back)
    back = lax.all_gather(back, FEAT, axis=0)
    back = total_of(back)
    total = jnp.sum(total.astype(F32), axis=0)
    return (total + dot_nn(back, down_right)).astype(BF16)


def solution(mesh):
    tok, feat = ("z", "yl"), FEAT
    inner = Mesh(mesh.devices.reshape(16, 2, 4, 2, 2), tok + feat)
    return jax.shard_map(
        per_device,
        mesh=inner,
        in_specs=(
            P(tok, feat),
            P(feat, tok, None, None),
            P(feat, tok, None, None),
            P(feat, None),
            P(feat, tok, None),
            P(feat, tok, None),
            P(None, feat),
        ),
        out_specs=P(tok, feat),
        check_vma=False,
    )
```
